256 devices in a mesh: row: 16 (over y, x), col: 16 (over z, core).
Axes of the slice: x: 4, y: 4, z: 8, core: 2. Of those that a mesh axis runs over, the one named last changes fastest.
Arguments:
- right_side: float32 [8192, 8192], P('row', 'col'), may hold values from -6 to 6
- upper_left: bfloat16 [8192, 8192], P('row', 'col'), may hold values from -0.1875 to 0.1875
- upper_right: bfloat16 [8192, 8192], P('row', 'col'), may hold values from -0.1875 to 0.1875
- vectors_left: bfloat16 [8192, 512], P('row'), may hold values from -1 to 1, as said below
- vectors_right: bfloat16 [8192, 512], P('col'), may hold values from -1 to 1, as said below
- values_left: float32 [8192], P('row'), may hold values from 0.5 to 1
- values_right: float32 [8192], P('col'), may hold values from 0.5 to 1
Outputs:
- progress: float32 [8192, 8192], P('row', 'col')
The draws below stay inside these ranges and needn't reach their ends.
Inputs may be any that keep to these rules, and one draw needn't show every extreme that they name: `vectors_left`: each block of 512 rows is an orthogonal matrix rounded to bfloat16. `vectors_right`: each block of 512 rows is an orthogonal matrix rounded to bfloat16.
All inputs are finite; a program needn't handle non-finite values.
Results may differ from the reference program's by a relative error of at most 0.023.
Values may be sent and summed in bfloat16 or wider, within the bound.
A program may use at most 128 MiB of HBM per device.

```python
import jax
import jax.numpy as jnp
from jax import lax

TILE = 512
STEPS = 8
ORDER_A = 8192
ORDER_B = 8192
N_ROW = 16
N_COL = 16


def orthogonal_tiles(key, number, length):
    indices = jnp.arange(length).astype(jnp.float32)
    cosines = jnp.cos(jnp.pi * (2.0 * indices[None, :] + 1.0) * indices[:, None] / (2.0 * length))
    weights = jnp.where(indices == 0.0, jnp.sqrt(1.0 / length), jnp.sqrt(2.0 / length))
    basis = cosines * weights[:, None]

    def single_tile(subkey):
        key_rows, key_cols, key_perm, key_mirror = jax.random.split(subkey, 4)
        signs_rows = jnp.where(jax.random.bernoulli(key_rows, 0.5, (length,)), 1.0, -1.0)
        signs_cols = jnp.where(jax.random.bernoulli(key_cols, 0.5, (length,)), 1.0, -1.0)
        shuffle = jax.random.permutation(key_perm, length)
        matrix = basis[shuffle] * signs_rows[:, None] * signs_cols[None, :]
        mirror = jax.random.normal(key_mirror, (length,), jnp.float32)
        matrix = matrix - 2.0 * jnp.outer(matrix @ mirror, mirror) / jnp.dot(mirror, mirror)
        return matrix
    subkeys = jax.random.split(key, number)
    tiles_all = jax.vmap(single_tile)(subkeys)
    return tiles_all.reshape(number * length, length).astype(jnp.bfloat16)


def draw_vectors_left(key, part):
    return orthogonal_tiles(jax.random.fold_in(key, 11), ORDER_A // TILE, TILE)


def draw_vectors_right(key, part):
    return orthogonal_tiles(jax.random.fold_in(key, 23), ORDER_B // TILE, TILE)


def block_levels(stream_key, dims, cuts, least, high):
    loudness, own = 1.0, jax.random.fold_in(stream_key, 6)
    for dim, blocks in cuts:
        heights = jnp.exp(jax.random.uniform(jax.random.fold_in(own, dim), (blocks,), jnp.float32, least / len(cuts), high / len(cuts)))
        loudness = loudness * jnp.repeat(heights, dims[dim] // blocks).reshape([-1 if axis == dim else 1 for axis in range(len(dims))])
    return loudness


def centred(own_key, extent, deviation, most, cuts=(), kind=jnp.bfloat16):
    values = jax.random.normal(own_key, extent, jnp.float32) * deviation
    if len(cuts) > 0:
        values = block_levels(own_key, extent, cuts, -0.22, 0.18) * values
    return jnp.clip(values, min=-most, max=most).astype(kind)


def setup_inputs(seed: int = 0) -> dict:
    key_list = jax.random.split(jax.random.key(seed), 8)
    return {
        "right_side": centred(key_list[0], (ORDER_A, ORDER_B), 1.0, 6.0, ((0, 16), (1, 16)), jnp.float32),
        "upper_left": centred(key_list[1], (ORDER_A, ORDER_A), (2 * TILE) ** -0.5, 0.1875, ((0, 16), (1, 16))),
        "upper_right": centred(key_list[2], (ORDER_B, ORDER_B), (2 * TILE) ** -0.5, 0.1875, ((0, 16), (1, 16))),
        "vectors_left": draw_vectors_left(jax.random.fold_in(key_list[7], 71), 0),
        "vectors_right": draw_vectors_right(jax.random.fold_in(key_list[7], 71), 0),
        "values_left": jnp.clip(0.5 + 0.5 * jax.random.uniform(key_list[5], (ORDER_A,), jnp.float32) ** block_levels(key_list[5], (ORDER_A,), ((0, 16),), -0.2, 0.2), 0.5, 1.0),
        "values_right": jnp.clip(0.5 + 0.5 * jax.random.uniform(key_list[6], (ORDER_B,), jnp.float32) ** block_levels(key_list[6], (ORDER_B,), ((0, 16),), -0.2, 0.2), 0.5, 1.0),
    }


def product(left_side, right_factor):
    left_side = lax.optimization_barrier(left_side)
    right_factor = lax.optimization_barrier(right_factor)
    return jnp.dot(left_side.astype(jnp.float32), right_factor.astype(jnp.float32), precision=lax.Precision.HIGHEST)


def solve_tile(remain, vec_left, vec_right, eigen_sums):
    halfway = product(vec_left.T, remain.astype(jnp.bfloat16)).astype(jnp.bfloat16)
    rotated = product(halfway, vec_right)
    scaled = (rotated / eigen_sums).astype(jnp.bfloat16)
    turned = product(vec_left, scaled).astype(jnp.bfloat16)
    return product(turned, vec_right.T)


def reference(right_side, upper_left, upper_right, vectors_left, vectors_right, values_left, values_right):
    current = right_side
    for section_index in range(STEPS):
        solved = []
        for column in range(N_COL):
            offset_lag = section_index - column
            if 0 <= offset_lag < N_ROW:
                row_index = N_ROW - 1 - offset_lag
                row_span = slice(row_index * TILE, (row_index + 1) * TILE)
                col_span = slice(column * TILE, (column + 1) * TILE)
                eigen_sums = values_left[row_span][:, None] + values_right[col_span][None, :]
                answer = solve_tile(current[row_span, col_span], vectors_left[row_span], vectors_right[col_span], eigen_sums)
                solved.append((row_index, column, answer))
        for row_index, column, answer in solved:
            row_span = slice(row_index * TILE, (row_index + 1) * TILE)
            col_span = slice(column * TILE, (column + 1) * TILE)
            current = current.at[row_span, col_span].set(answer)
            rounded = answer.astype(jnp.bfloat16)
            if row_index > 0:
                update = product(upper_left[: row_index * TILE, row_span], rounded)
                current = current.at[: row_index * TILE, col_span].add(-update)
            if column < N_COL - 1:
                update = product(rounded, upper_right[col_span, (column + 1) * TILE:])
                current = current.at[row_span, (column + 1) * TILE:].add(-update)
    return current
```

```python
import jax
import jax.numpy as jnp
from jax import lax
from jax.experimental import pallas as pl
from jax.experimental.pallas import tpu as pltpu
from jax.sharding import PartitionSpec as P

STEPS = 8
SIDE = 16
CHUNKS = 4
MESH = pl.DeviceIdType.MESH
BF16 = jnp.bfloat16
F32 = jnp.float32


def column_edges():
    edges = set()
    for chip in range(8):
        edges.add((2 * chip, 2 * chip + 1))
        if chip < 7:
            edges.add((2 * chip, 2 * chip + 2))
            edges.add((2 * chip + 1, 2 * chip + 2))
    edges |= {(0, far) for far in range(12, 16)}
    edges |= {(6, far) for far in range(8, 12)}
    edges |= {(2, 6), (0, 2)}
    edges |= {(far - 1, far) for far in range(9, 16)}
    return edges


def dot(left, right):
    return jnp.dot(left, right, preferred_element_type=F32)


def kernel(
    c_ref, a_ref, b_ref, u_ref, v_ref, al_ref, bl_ref, o_ref,
    ut, vt, inv, hbuf, ybuf, solved, xcol, xrow, abuf, bbuf,
    col_recv, row_recv, a_recv, b_recv,
    col_send, row_send, a_send, b_send, token,
):
    row = lax.axis_index("row")
    col = lax.axis_index("col")
    lag = SIDE - 1 - row
    x = row % 4
    y = row // 4
    even = col % 2 == 0
    size = c_ref.shape[0]
    part = size // CHUNKS
    parts = [pl.ds(p * part, part) for p in range(CHUNKS)]

    def row_of(x_to, y_to):
        return ((y_to + 4) % 4) * 4 + (x_to + 4) % 4

    x_minus, x_plus = row_of(x - 1, y), row_of(x + 1, y)
    y_minus, y_plus = row_of(x, y - 1), row_of(x, y + 1)

    def copy(src, dst, send, recv, to_row, to_col):
        return pltpu.make_async_remote_copy(
            src_ref=src, dst_ref=dst, send_sem=send, recv_sem=recv,
            device_id=(to_row, to_col), device_id_type=MESH,
        )

    def received(dst, recv):
        copy(dst, dst, recv, recv, row, col).wait_recv()

    barrier = pltpu.get_barrier_semaphore()
    for near in (x_minus, x_plus, y_minus, y_plus):
        pl.semaphore_signal(barrier, inc=1, device_id=(near, col), device_id_type=MESH)
    count = jnp.int32(4)
    edges = column_edges()
    for other in range(SIDE):
        near = sorted({b for a, b in edges if a == other} | {a for a, b in edges if b == other})
        hit = col == near[0]
        for mine in near[1:]:
            hit = hit | (col == mine)

        @pl.when(hit)
        def _():
            pl.semaphore_signal(barrier, inc=1, device_id=(row, other), device_id_type=MESH)

        count = count + hit.astype(jnp.int32)
    pl.semaphore_wait(barrier, count)

    def a_children(t):
        mine = lag > t
        last = STEPS - 1 - t
        onward = even & (t < 4) & (col + 2 <= last)
        back = (t >= 4) & ((col == 6) | (col == 2))
        side = even & (col + 1 <= last)
        return [
            (mine & (onward | back), row, jnp.where(onward, col + 2, jnp.where(col == 6, 2, 0))),
            (mine & side, row, jnp.minimum(col + 1, SIDE - 1)),
        ]

    def a_receives(t):
        return (lag > t) & ((col <= STEPS - 1 - t) | ((t >= 4) & ((col == 6) | (col == 2))))

    def b_children(k):
        xs = k % 4
        low = k < 4
        d = (xs - x + 4) % 4
        ring = low & (y == 3)
        start_low = low & (y == 0) & (x == xs)
        up = (start_low | (low & (y == 1) & (x == xs))) | (
            (~low) & ((y == 1) | (y == 2)) & (x == xs)
        )
        forward = (low & (y == 2) & (x >= xs) & (x < 3)) | (
            (~low) & (y == 3) & (x >= xs) & (x < 3)
        )
        mine = col > k
        return [
            (mine & start_low, y_minus, col),
            (mine & up, y_plus, col),
            (mine & ring & (d <= 1), x_minus, col),
            (mine & ((ring & (d == 0)) | forward), x_plus, col),
        ]

    def b_receives(k):
        xs = k % 4
        low = k < 4
        return (col > k) & (
            (low & ((y == 3) | ((y == 1) & (x == xs)) | ((y == 2) & (x >= xs))))
            | ((~low) & (((y == 2) & (x == xs)) | ((y == 3) & (x >= xs))))
        )

    def col_children(lk):
        rk = SIDE - 1 - lk
        xk, yk = rk % 4, rk // 4
        d = (xk - x + 4) % 4
        own = y == yk
        return [
            (own & (d <= 1), x_minus, col),
            (own & (d == 0), x_plus, col),
            ((own & (yk == 3)) | ((yk == 2) & ((y == 2) | (y == 1))), y_minus, col),
            ((yk == 3) & ((y == 3) | (y == 0)), y_plus, col),
        ]

    def row_children(k):
        return [
            (even & (col < SIDE - 1), row, jnp.minimum(col + 1, SIDE - 1)),
            ((col < SIDE - 2) & (even | (col == k)), row, jnp.minimum((col // 2 + 1) * 2, SIDE - 1)),
        ]

    def send_all(children, src, dst, sends, recv, where=True):
        for index, (condition, to_row, to_col) in enumerate(children):
            @pl.when(condition & where)
            def _():
                copy(src, dst, sends.at[index], recv, to_row, to_col).start()

    def sent_all(children, whole, sends, where=True):
        for index, (condition, to_row, to_col) in enumerate(children):
            @pl.when(condition & where)
            def _():
                copy(whole, whole, sends.at[index], sends.at[index], row, col).wait_send()

    is_b_source = (row < STEPS) & (col > row)
    b_own = jnp.minimum(row, STEPS - 1)
    send_all(b_children(b_own), b_ref, bbuf.at[b_own], b_send.at[b_own], b_recv.at[b_own], is_b_source)

    def a_source(t):
        mine = (col == SIDE - 1 - t) & (lag > t)
        first = (t == 0) | (t == 4)
        target = jnp.where(t < 4, 0, 6)
        this = copy(a_ref, abuf.at[t], a_send.at[t, 2], a_recv.at[t], row, target)

        @pl.when(mine & ~first)
        def _():
            pl.semaphore_wait(token, 1)

        @pl.when(mine)
        def _():
            this.start()
            this.wait_send()

        @pl.when(mine & (t != 3) & (t != 7) & (lag > t + 1))
        def _():
            pl.semaphore_signal(token, inc=1, device_id=(row, col - 1), device_id_type=MESH)

    a_source(jnp.int32(0))
    a_source(jnp.int32(4))

    ut[...] = u_ref[...].astype(F32).T.astype(BF16)
    vt[...] = v_ref[...].astype(F32).T.astype(BF16)
    sums = jnp.broadcast_to(al_ref[...], (size, size)).T + jnp.broadcast_to(bl_ref[...], (size, size))
    inv[...] = 1.0 / sums
    o_ref[...] = c_ref[...]

    def step(s, carry):
        a_in = a_receives(s)

        @pl.when(a_in)
        def _():
            received(abuf.at[s], a_recv.at[s])
            send_all(a_children(s), abuf.at[s], abuf.at[s], a_send.at[s], a_recv.at[s])

        @pl.when(s < 3)
        def _():
            a_source(s + 1)
            a_source(s + 5)

        @pl.when(b_receives(s))
        def _():
            received(bbuf.at[s], b_recv.at[s])
            send_all(b_children(s), bbuf.at[s], bbuf.at[s], b_send.at[s], b_recv.at[s])

        lk = s - col
        k = s - lag
        lk_at, k_at = jnp.maximum(lk, 0), jnp.maximum(k, 0)
        mine = lag + col == s
        from_col = (lk >= 0) & (lag != lk) & ((lk < 4) | (y < 3))
        from_row = (k >= 0) & (col > k)
        use_col = (lk >= 0) & (lag > lk)

        @pl.when(mine)
        def _():
            rounded = o_ref[...].astype(BF16)
            hbuf[...] = dot(ut[...], rounded).astype(BF16)
            ybuf[...] = (dot(hbuf[...], v_ref[...]) * inv[...]).astype(BF16)
            for rows in parts:
                turned = dot(u_ref[rows, :], ybuf[...]).astype(BF16)
                answer = dot(turned, vt[...])
                o_ref[rows, :] = answer
                solved[rows, :] = answer.astype(BF16)
                p = parts.index(rows)
                src = solved.at[rows]
                send_all(
                    col_children(lk_at), src, xcol.at[lk_at, rows], col_send.at[lk_at],
                    col_recv.at[lk_at, p],
                )
                send_all(
                    row_children(k_at), src, xrow.at[k_at, rows], row_send.at[k_at],
                    row_recv.at[k_at, p],
                )

        for p, rows in enumerate(parts):
            @pl.when(from_col)
            def _():
                tile = xcol.at[lk_at, rows]
                received(tile, col_recv.at[lk_at, p])
                send_all(col_children(lk_at), tile, tile, col_send.at[lk_at], col_recv.at[lk_at, p])

            @pl.when(from_row)
            def _():
                tile = xrow.at[k_at, rows]
                received(tile, row_recv.at[k_at, p])
                send_all(row_children(k_at), tile, tile, row_send.at[k_at], row_recv.at[k_at, p])

            @pl.when(use_col)
            def _():
                o_ref[...] -= dot(abuf[lk_at, :, rows], xcol[lk_at, rows, :])

            @pl.when(from_row)
            def _():
                o_ref[rows, :] -= dot(xrow[k_at, rows, :], bbuf[k_at])

        return carry

    lax.fori_loop(0, STEPS, step, 0)

    send_b = is_b_source
    sent_all(b_children(b_own), bbuf.at[b_own], b_send.at[b_own], send_b)

    def drain(s, carry):
        sent_all(a_children(s), abuf.at[s], a_send.at[s], a_receives(s))
        sent_all(b_children(s), bbuf.at[s], b_send.at[s], b_receives(s))
        lk = s - col
        k = s - lag
        lk_at, k_at = jnp.maximum(lk, 0), jnp.maximum(k, 0)
        source = lag + col == s
        from_col = (lk >= 0) & ((lk < 4) | (y < 3))
        from_row = (k >= 0) & (col >= k)
        sent_all(col_children(lk_at), xcol.at[lk_at], col_send.at[lk_at], from_col)
        sent_all(row_children(k_at), xrow.at[k_at], row_send.at[k_at], from_row)
        return carry

    lax.fori_loop(0, STEPS, drain, 0)


def per_device(right_side, upper_left, upper_right, vectors_left, vectors_right, values_left, values_right):
    size = right_side.shape[0]
    tile = pltpu.VMEM((size, size), BF16)
    tiles = pltpu.VMEM((STEPS, size, size), BF16)
    sems = pltpu.SemaphoreType.DMA
    vmem = pl.BlockSpec(memory_space=pltpu.VMEM)
    return pl.pallas_call(
        kernel,
        out_shape=jax.ShapeDtypeStruct((size, size), F32),
        in_specs=[vmem] * 7,
        out_specs=vmem,
        scratch_shapes=[
            tile, tile, pltpu.VMEM((size, size), F32), tile, tile, tile,
            tiles, tiles, tiles, tiles,
            sems((STEPS, CHUNKS)), sems((STEPS, CHUNKS)), sems((STEPS,)), sems((STEPS,)),
            sems((STEPS, 4)), sems((STEPS, 2)), sems((STEPS, 3)), sems((STEPS, 4)),
            pltpu.SemaphoreType.REGULAR,
        ],
        compiler_params=pltpu.CompilerParams(
            collective_id=0, has_side_effects=True, vmem_limit_bytes=48 << 20
        ),
        name="sylvester",
    )(
        right_side, upper_left, upper_right, vectors_left, vectors_right,
        values_left.reshape(1, size), values_right.reshape(1, size),
    )


def solution(mesh):
    in_specs = (
        P("row", "col"),
        P("row", "col"),
        P("row", "col"),
        P("row", None),
        P("col", None),
        P("row"),
        P("col"),
    )
    return jax.shard_map(
        per_device, mesh=mesh, in_specs=in_specs, out_specs=P("row", "col"), check_vma=False
    )
```

```python
import jax
import jax.numpy as jnp
from jax import lax
from jax.experimental import pallas as pl
from jax.experimental.pallas import tpu as pltpu
from jax.sharding import PartitionSpec as P

STEPS = 8
SIDE = 16
CHUNKS = 4
MESH = pl.DeviceIdType.MESH
BF16 = jnp.bfloat16
F32 = jnp.float32


def column_edges():
    edges = set()
    for chip in range(8):
        edges.add((2 * chip, 2 * chip + 1))
        if chip < 7:
            edges.add((2 * chip, 2 * chip + 2))
            edges.add((2 * chip + 1, 2 * chip + 2))
    edges |= {(0, far) for far in range(12, 16)}
    edges |= {(6, far) for far in range(8, 12)}
    edges |= {(2, 6), (0, 2)}
    edges |= {(far - 1, far) for far in range(9, 16)}
    return edges


def dot(left, right):
    return jnp.dot(left, right, preferred_element_type=F32)


def kernel(
    c_any, a_any, b_any, u_any, v_any, al_any, bl_any, o_ref,
    u_ref, v_ref, al_ref, bl_ref,
    ut, vt, inv, hbuf, ybuf, solved, xcol, xrow, abuf, bbuf,
    col_recv, row_recv, a_recv, b_recv,
    col_send, row_send, a_send, b_send, a_first, loaded, token,
):
    row = lax.axis_index("row")
    col = lax.axis_index("col")
    lag = SIDE - 1 - row
    x = row % 4
    y = row // 4
    even = col % 2 == 0
    size = o_ref.shape[0]
    part = size // CHUNKS
    parts = [pl.ds(p * part, part) for p in range(CHUNKS)]

    def row_of(x_to, y_to):
        return ((y_to + 4) % 4) * 4 + (x_to + 4) % 4

    x_minus, x_plus = row_of(x - 1, y), row_of(x + 1, y)
    y_minus, y_plus = row_of(x, y - 1), row_of(x, y + 1)

    def copy(src, dst, send, recv, to_row, to_col):
        return pltpu.make_async_remote_copy(
            src_ref=src, dst_ref=dst, send_sem=send, recv_sem=recv,
            device_id=(to_row, to_col), device_id_type=MESH,
        )

    def received(dst, recv):
        copy(dst, dst, recv, recv, row, col).wait_recv()

    loads = [
        pltpu.make_async_copy(src, dst, loaded.at[index])
        for index, (src, dst) in enumerate(
            [(c_any, o_ref), (u_any, u_ref), (v_any, v_ref), (al_any, al_ref), (bl_any, bl_ref)]
        )
    ]
    for load in loads:
        load.start()

    barrier = pltpu.get_barrier_semaphore()
    for near in (x_minus, x_plus, y_minus, y_plus):
        pl.semaphore_signal(barrier, inc=1, device_id=(near, col), device_id_type=MESH)
    count = jnp.int32(4)
    edges = column_edges()
    for other in range(SIDE):
        near = sorted({b for a, b in edges if a == other} | {a for a, b in edges if b == other})
        hit = col == near[0]
        for mine in near[1:]:
            hit = hit | (col == mine)

        @pl.when(hit)
        def _():
            pl.semaphore_signal(barrier, inc=1, device_id=(row, other), device_id_type=MESH)

        count = count + hit.astype(jnp.int32)
    pl.semaphore_wait(barrier, count)

    def a_children(t):
        mine = lag > t
        last = STEPS - 1 - t
        onward = even & (t < 4) & (col + 2 <= last)
        back = (t >= 4) & ((col == 6) | (col == 2))
        side = even & (col + 1 <= last)
        return [
            (mine & (onward | back), row, jnp.where(onward, col + 2, jnp.where(col == 6, 2, 0))),
            (mine & side, row, jnp.minimum(col + 1, SIDE - 1)),
        ]

    def a_receives(t):
        return (lag > t) & ((col <= STEPS - 1 - t) | ((t >= 4) & ((col == 6) | (col == 2))))

    def b_children(k):
        xs = k % 4
        low = k < 4
        d = (xs - x + 4) % 4
        ring = low & (y == 3)
        start_low = low & (y == 0) & (x == xs)
        up = (start_low | (low & (y == 1) & (x == xs))) | (
            (~low) & ((y == 1) | (y == 2)) & (x == xs)
        )
        forward = (low & (y == 2) & (x >= xs) & (x < 3)) | (
            (~low) & (y == 3) & (x >= xs) & (x < 3)
        )
        mine = col > k
        return [
            (mine & start_low, y_minus, col),
            (mine & up, y_plus, col),
            (mine & ring & (d <= 1), x_minus, col),
            (mine & ((ring & (d == 0)) | forward), x_plus, col),
        ]

    def b_receives(k):
        xs = k % 4
        low = k < 4
        return (col > k) & (
            (low & ((y == 3) | ((y == 1) & (x == xs)) | ((y == 2) & (x >= xs))))
            | ((~low) & (((y == 2) & (x == xs)) | ((y == 3) & (x >= xs))))
        )

    def col_children(lk):
        rk = SIDE - 1 - lk
        xk, yk = rk % 4, rk // 4
        d = (xk - x + 4) % 4
        own = y == yk
        return [
            (own & (d <= 1), x_minus, col),
            (own & (d == 0), x_plus, col),
            ((own & (yk == 3)) | ((yk == 2) & ((y == 2) | (y == 1))), y_minus, col),
            ((yk == 3) & ((y == 3) | (y == 0)), y_plus, col),
        ]

    def row_children(k):
        return [
            (even & (col < SIDE - 1), row, jnp.minimum(col + 1, SIDE - 1)),
            ((col < SIDE - 2) & (even | (col == k)), row, jnp.minimum((col // 2 + 1) * 2, SIDE - 1)),
        ]

    def send_all(children, src, dst, sends, recv, where=True):
        for index, (condition, to_row, to_col) in enumerate(children):
            @pl.when(condition & where)
            def _():
                copy(src, dst, sends.at[index], recv, to_row, to_col).start()

    def sent_all(children, whole, sends, where=True):
        for index, (condition, to_row, to_col) in enumerate(children):
            @pl.when(condition & where)
            def _():
                copy(whole, whole, sends.at[index], sends.at[index], row, col).wait_send()

    is_b_source = (row < STEPS) & (col > row)
    b_own = jnp.minimum(row, STEPS - 1)
    for p, rows in enumerate(parts):
        send_all(
            b_children(b_own), b_any.at[rows], bbuf.at[b_own, rows], b_send.at[b_own],
            b_recv.at[b_own, p], is_b_source,
        )

    t_own = jnp.minimum(SIDE - 1 - col, STEPS - 1)
    is_a_source = (col >= SIDE - STEPS) & (lag > t_own)
    a_target = jnp.where(t_own < 4, 0, 6)
    a_copies = [
        copy(
            a_any.at[rows], abuf.at[t_own, rows], a_first.at[p], a_recv.at[t_own, p], row, a_target
        )
        for p, rows in enumerate(parts)
    ]

    @pl.when(is_a_source & (t_own != 0) & (t_own != 4))
    def _():
        pl.semaphore_wait(token, 1)

    @pl.when(is_a_source)
    def _():
        for this in a_copies:
            this.start()
        for this in a_copies[:-1]:
            this.wait_send()

    @pl.when(is_a_source & (t_own != 3) & (t_own != 7) & (lag > t_own + 1))
    def _():
        pl.semaphore_signal(token, inc=1, device_id=(row, col - 1), device_id_type=MESH)

    for load in loads:
        load.wait()
    ut[...] = u_ref[...].astype(F32).T.astype(BF16)
    vt[...] = v_ref[...].astype(F32).T.astype(BF16)
    sums = jnp.broadcast_to(al_ref[...], (size, size)).T + jnp.broadcast_to(bl_ref[...], (size, size))
    inv[...] = 1.0 / sums

    def step(s, carry):
        for p, rows in enumerate(parts):
            @pl.when(a_receives(s))
            def _():
                tile = abuf.at[s, rows]
                received(tile, a_recv.at[s, p])
                send_all(a_children(s), tile, tile, a_send.at[s], a_recv.at[s, p])

        for p, rows in enumerate(parts):
            @pl.when(b_receives(s))
            def _():
                tile = bbuf.at[s, rows]
                received(tile, b_recv.at[s, p])
                send_all(b_children(s), tile, tile, b_send.at[s], b_recv.at[s, p])

        lk = s - col
        k = s - lag
        lk_at, k_at = jnp.maximum(lk, 0), jnp.maximum(k, 0)
        mine = lag + col == s
        from_col = (lk >= 0) & (lag != lk) & ((lk < 4) | (y < 3))
        from_row = (k >= 0) & (col > k)
        use_col = (lk >= 0) & (lag > lk)

        @pl.when(mine)
        def _():
            rounded = o_ref[...].astype(BF16)
            hbuf[...] = dot(ut[...], rounded).astype(BF16)
            ybuf[...] = (dot(hbuf[...], v_ref[...]) * inv[...]).astype(BF16)
            for rows in parts:
                turned = dot(u_ref[rows, :], ybuf[...]).astype(BF16)
                answer = dot(turned, vt[...])
                o_ref[rows, :] = answer
                solved[rows, :] = answer.astype(BF16)
                p = parts.index(rows)
                src = solved.at[rows]
                send_all(
                    col_children(lk_at), src, xcol.at[lk_at, rows], col_send.at[lk_at],
                    col_recv.at[lk_at, p],
                )
                send_all(
                    row_children(k_at), src, xrow.at[k_at, rows], row_send.at[k_at],
                    row_recv.at[k_at, p],
                )

        for p, rows in enumerate(parts):
            @pl.when(from_col)
            def _():
                tile = xcol.at[lk_at, rows]
                received(tile, col_recv.at[lk_at, p])
                send_all(col_children(lk_at), tile, tile, col_send.at[lk_at], col_recv.at[lk_at, p])

            @pl.when(from_row)
            def _():
                tile = xrow.at[k_at, rows]
                received(tile, row_recv.at[k_at, p])
                send_all(row_children(k_at), tile, tile, row_send.at[k_at], row_recv.at[k_at, p])

            @pl.when(use_col)
            def _():
                o_ref[...] -= dot(abuf[lk_at, :, rows], xcol[lk_at, rows, :])

            @pl.when(from_row)
            def _():
                o_ref[rows, :] -= dot(xrow[k_at, rows, :], bbuf[k_at])

        return carry

    lax.fori_loop(0, STEPS, step, 0)

    sent_all(b_children(b_own), bbuf.at[b_own], b_send.at[b_own], is_b_source)

    @pl.when(is_a_source)
    def _():
        a_copies[-1].wait_send()

    def drain(s, carry):
        sent_all(a_children(s), abuf.at[s], a_send.at[s], a_receives(s))
        sent_all(b_children(s), bbuf.at[s], b_send.at[s], b_receives(s))
        lk = s - col
        k = s - lag
        lk_at, k_at = jnp.maximum(lk, 0), jnp.maximum(k, 0)
        source = lag + col == s
        from_col = (lk >= 0) & ((lk < 4) | (y < 3))
        from_row = (k >= 0) & (col >= k)
        sent_all(col_children(lk_at), xcol.at[lk_at], col_send.at[lk_at], from_col)
        sent_all(row_children(k_at), xrow.at[k_at], row_send.at[k_at], from_row)
        return carry

    lax.fori_loop(0, STEPS, drain, 0)


def per_device(right_side, upper_left, upper_right, vectors_left, vectors_right, values_left, values_right):
    size = right_side.shape[0]
    tile = pltpu.VMEM((size, size), BF16)
    tiles = pltpu.VMEM((STEPS, size, size), BF16)
    sems = pltpu.SemaphoreType.DMA
    vmem = pl.BlockSpec(memory_space=pltpu.VMEM)
    return pl.pallas_call(
        kernel,
        out_shape=jax.ShapeDtypeStruct((size, size), F32),
        in_specs=[pl.BlockSpec(memory_space=pl.ANY)] * 7,
        out_specs=vmem,
        scratch_shapes=[
            tile, tile, pltpu.VMEM((1, size), F32), pltpu.VMEM((1, size), F32),
            tile, tile, pltpu.VMEM((size, size), F32), tile, tile, tile,
            tiles, tiles, tiles, tiles,
            sems((STEPS, CHUNKS)), sems((STEPS, CHUNKS)), sems((STEPS, CHUNKS)), sems((STEPS, CHUNKS)),
            sems((STEPS, 4)), sems((STEPS, 2)), sems((STEPS, 2)), sems((STEPS, 4)),
            sems((CHUNKS,)), sems((5,)),
            pltpu.SemaphoreType.REGULAR,
        ],
        compiler_params=pltpu.CompilerParams(
            collective_id=0, has_side_effects=True, vmem_limit_bytes=48 << 20
        ),
        name="sylvester",
    )(
        right_side, upper_left, upper_right, vectors_left, vectors_right,
        values_left.reshape(1, size), values_right.reshape(1, size),
    )


def solution(mesh):
    in_specs = (
        P("row", "col"),
        P("row", "col"),
        P("row", "col"),
        P("row", None),
        P("col", None),
        P("row"),
        P("col"),
    )
    return jax.shard_map(
        per_device, mesh=mesh, in_specs=in_specs, out_specs=P("row", "col"), check_vma=False
    )
```

```python
import jax
import jax.numpy as jnp
from jax import lax
from jax.experimental import pallas as pl
from jax.experimental.pallas import tpu as pltpu
from jax.sharding import PartitionSpec as P

STEPS = 8
SIDE = 16
CHUNKS = 4
MESH = pl.DeviceIdType.MESH
BF16 = jnp.bfloat16
F32 = jnp.float32


def column_edges():
    edges = set()
    for chip in range(8):
        edges.add((2 * chip, 2 * chip + 1))
        if chip < 7:
            edges.add((2 * chip, 2 * chip + 2))
            edges.add((2 * chip + 1, 2 * chip + 2))
    edges |= {(0, far) for far in range(12, 16)}
    edges |= {(2, far) for far in range(8, 12)}
    edges |= {(0, 2)}
    edges |= {(far - 1, far) for far in range(9, 16)}
    return edges


def dot(left, right):
    return jnp.dot(left, right, preferred_element_type=F32)


def kernel(
    c_any, a_any, b_any, u_any, v_any, al_any, bl_any, o_ref,
    u_ref, v_ref, al_ref, bl_ref,
    ut, vt, inv, hbuf, ybuf, solved, xcol, xrow, abuf, bbuf,
    col_recv, row_recv, a_recv, b_recv,
    col_send, row_send, a_send, b_send, a_first, loaded, token,
):
    row = lax.axis_index("row")
    col = lax.axis_index("col")
    lag = SIDE - 1 - row
    x = row % 4
    y = row // 4
    even = col % 2 == 0
    size = o_ref.shape[0]
    part = size // CHUNKS
    parts = [pl.ds(p * part, part) for p in range(CHUNKS)]

    def row_of(x_to, y_to):
        return ((y_to + 4) % 4) * 4 + (x_to + 4) % 4

    x_minus, x_plus = row_of(x - 1, y), row_of(x + 1, y)
    y_minus, y_plus = row_of(x, y - 1), row_of(x, y + 1)

    def copy(src, dst, send, recv, to_row, to_col):
        return pltpu.make_async_remote_copy(
            src_ref=src, dst_ref=dst, send_sem=send, recv_sem=recv,
            device_id=(to_row, to_col), device_id_type=MESH,
        )

    def received(dst, recv):
        copy(dst, dst, recv, recv, row, col).wait_recv()

    loads = [
        pltpu.make_async_copy(src, dst, loaded.at[index])
        for index, (src, dst) in enumerate(
            [(c_any, o_ref), (u_any, u_ref), (v_any, v_ref), (al_any, al_ref), (bl_any, bl_ref)]
        )
    ]
    for load in loads:
        load.start()

    barrier = pltpu.get_barrier_semaphore()
    for near in (x_minus, x_plus, y_minus, y_plus):
        pl.semaphore_signal(barrier, inc=1, device_id=(near, col), device_id_type=MESH)
    for mine, other in ((12, 11), (11, 12)):
        @pl.when(row == mine)
        def _():
            pl.semaphore_signal(barrier, inc=1, device_id=(other, col), device_id_type=MESH)
    count = 4 + ((row == 11) | (row == 12)).astype(jnp.int32)
    edges = column_edges()
    for other in range(SIDE):
        near = sorted({b for a, b in edges if a == other} | {a for a, b in edges if b == other})
        hit = col == near[0]
        for mine in near[1:]:
            hit = hit | (col == mine)

        @pl.when(hit)
        def _():
            pl.semaphore_signal(barrier, inc=1, device_id=(row, other), device_id_type=MESH)

        count = count + hit.astype(jnp.int32)
    pl.semaphore_wait(barrier, count)

    def a_children(t):
        mine = lag > t
        last = STEPS - 1 - t
        onward = even & (t < 4) & (col + 2 <= last)
        back = (t >= 4) & (col == 2)
        side = even & (col + 1 <= last)
        return [
            (mine & (onward | back), row, jnp.where(onward, col + 2, 0)),
            (mine & side, row, jnp.minimum(col + 1, SIDE - 1)),
        ]

    def a_receives(t):
        return (lag > t) & ((col <= STEPS - 1 - t) | ((t >= 4) & (col == 2)))

    def b_children(k):
        xs = k % 4
        low = k < 4
        high = ~low
        right = x >= xs
        d = (xs - x + 4) % 4
        up, down = high & (k % 2 == 0), high & (k % 2 == 1)
        mine = col > k
        return [
            (mine & ((low & (y == 0)) | (down & right & ((y == 1) | (y == 0)))), y_minus, col),
            (
                mine & right & ((low & ((y == 0) | (y == 1))) | (up & ((y == 1) | (y == 2)))),
                y_plus, col,
            ),
            (mine & low & (y == 0) & (d == 0), x_minus, col),
            (
                mine & ((low & (y == 0) & ((d == 0) | (d == 3))) | (high & (y == 1) & right & (x < 3))),
                x_plus, col,
            ),
        ]

    def b_receives(k):
        right = x >= k % 4
        low = k < 4
        across = jnp.where(k % 2 == 0, 2, 0)
        return (col > k) & (row != k) & (
            (low & ((y == 3) | (y == 0) | right))
            | ((~low) & right & ((y == 1) | (y == 3) | (y == across)))
        )

    def col_children(lk):
        rk = SIDE - 1 - lk
        xk, yk = rk % 4, rk // 4
        d = (xk - x + 4) % 4
        own = y == yk
        return [
            (own & (d == 0), x_minus, col),
            (own & (d == 0) & (lk == 3), row_of(3, 2), col),
            (own & ((d == 0) | (d == 3)), x_plus, col),
            (
                (own & (yk == 3) & ((lk != 3) | (x != 3))) | ((yk == 2) & ((y == 2) | (y == 1))),
                y_minus, col,
            ),
            ((yk == 3) & ((y == 3) | (y == 0)), y_plus, col),
        ]

    def row_children(k):
        return [
            (even & (col < SIDE - 1), row, jnp.minimum(col + 1, SIDE - 1)),
            ((col < SIDE - 2) & (even | (col == k)), row, jnp.minimum((col // 2 + 1) * 2, SIDE - 1)),
        ]

    def send_all(children, src, dst, sends, recv, where=True):
        for index, (condition, to_row, to_col) in enumerate(children):
            @pl.when(condition & where)
            def _():
                copy(src, dst, sends.at[index], recv, to_row, to_col).start()

    def sent_all(children, whole, sends, where=True):
        for index, (condition, to_row, to_col) in enumerate(children):
            @pl.when(condition & where)
            def _():
                copy(whole, whole, sends.at[index], sends.at[index], row, col).wait_send()

    is_b_source = (row < STEPS) & (col > row)
    b_own = jnp.minimum(row, STEPS - 1)
    for p, rows in enumerate(parts):
        send_all(
            b_children(b_own), b_any.at[rows], bbuf.at[b_own, rows], b_send.at[b_own],
            b_recv.at[b_own, p], is_b_source,
        )

    t_own = jnp.minimum(SIDE - 1 - col, STEPS - 1)
    is_a_source = (col >= SIDE - STEPS) & (lag > t_own)
    a_target = jnp.where(t_own < 4, 0, 2)
    a_copies = [
        copy(
            a_any.at[rows], abuf.at[t_own, rows], a_first.at[p], a_recv.at[t_own, p], row, a_target
        )
        for p, rows in enumerate(parts)
    ]

    @pl.when(is_a_source & (t_own != 0) & (t_own != 4))
    def _():
        pl.semaphore_wait(token, 1)

    @pl.when(is_a_source)
    def _():
        for this in a_copies:
            this.start()
        for this in a_copies[:-1]:
            this.wait_send()

    @pl.when(is_a_source & (t_own != 3) & (t_own != 7) & (lag > t_own + 1))
    def _():
        pl.semaphore_signal(token, inc=1, device_id=(row, col - 1), device_id_type=MESH)

    for load in loads:
        load.wait()
    ut[...] = u_ref[...].astype(F32).T.astype(BF16)
    vt[...] = v_ref[...].astype(F32).T.astype(BF16)
    sums = jnp.broadcast_to(al_ref[...], (size, size)).T + jnp.broadcast_to(bl_ref[...], (size, size))
    inv[...] = 1.0 / sums

    def take_b(k, carry):
        for p, rows in enumerate(parts):
            @pl.when(b_receives(k) & ((y < 2) | ((y == 2) & (k > 3))))
            def _():
                tile = bbuf.at[k, rows]
                received(tile, b_recv.at[k, p])
                send_all(b_children(k), tile, tile, b_send.at[k], b_recv.at[k, p])

        return carry

    lax.fori_loop(0, STEPS, take_b, 0)

    def step(s, carry):
        first = jnp.where(s == 0, 0, jnp.where(s < 3, s + 1, jnp.minimum(s + 3, STEPS - 1)))
        second = jnp.where(s == 0, 1, jnp.minimum(s + 3, STEPS - 1))
        for t, here in ((first, s < 5), (second, s < 3)):
            for p, rows in enumerate(parts):
                @pl.when(here & even & a_receives(t))
                def _():
                    tile = abuf.at[t, rows]
                    received(tile, a_recv.at[t, p])
                    send_all(a_children(t), tile, tile, a_send.at[t], a_recv.at[t, p])

        lk = s - col
        k = s - lag
        lk_at, k_at = jnp.maximum(lk, 0), jnp.maximum(k, 0)
        mine = lag + col == s
        from_col = (lk >= 0) & (lag != lk) & ((lk < 4) | (y < 3))
        from_row = (k >= 0) & (col > k)
        use_col = (lk >= 0) & (lag > lk)

        @pl.when(mine)
        def _():
            rounded = o_ref[...].astype(BF16)
            hbuf[...] = dot(ut[...], rounded).astype(BF16)
            ybuf[...] = (dot(hbuf[...], v_ref[...]) * inv[...]).astype(BF16)
            for rows in parts:
                turned = dot(u_ref[rows, :], ybuf[...]).astype(BF16)
                answer = dot(turned, vt[...])
                o_ref[rows, :] = answer
                solved[rows, :] = answer.astype(BF16)
                p = parts.index(rows)
                src = solved.at[rows]
                send_all(
                    col_children(lk_at), src, xcol.at[lk_at, rows], col_send.at[lk_at],
                    col_recv.at[lk_at, p],
                )
                send_all(
                    row_children(k_at), src, xrow.at[k_at, rows], row_send.at[k_at],
                    row_recv.at[k_at, p],
                )

        for p, rows in enumerate(parts):
            @pl.when(from_row)
            def _():
                tile = xrow.at[k_at, rows]
                received(tile, row_recv.at[k_at, p])
                send_all(row_children(k_at), tile, tile, row_send.at[k_at], row_recv.at[k_at, p])

        for p, rows in enumerate(parts):
            @pl.when(from_row)
            def _():
                received(bbuf.at[k_at, rows], b_recv.at[k_at, p])

            @pl.when(use_col & ~even)
            def _():
                received(abuf.at[lk_at, rows], a_recv.at[lk_at, p])

        for p, rows in enumerate(parts):
            @pl.when(from_row)
            def _():
                o_ref[rows, :] -= dot(xrow[k_at, rows, :], bbuf[k_at])

            @pl.when(from_col)
            def _():
                tile = xcol.at[lk_at, rows]
                received(tile, col_recv.at[lk_at, p])
                send_all(col_children(lk_at), tile, tile, col_send.at[lk_at], col_recv.at[lk_at, p])

            @pl.when(use_col)
            def _():
                o_ref[...] -= dot(abuf[lk_at, :, rows], xcol[lk_at, rows, :])

        return carry

    lax.fori_loop(0, STEPS, step, 0)

    sent_all(b_children(b_own), bbuf.at[b_own], b_send.at[b_own], is_b_source)

    @pl.when(is_a_source)
    def _():
        a_copies[-1].wait_send()

    def drain(s, carry):
        sent_all(a_children(s), abuf.at[s], a_send.at[s], a_receives(s))
        sent_all(b_children(s), bbuf.at[s], b_send.at[s], b_receives(s))
        lk = s - col
        k = s - lag
        lk_at, k_at = jnp.maximum(lk, 0), jnp.maximum(k, 0)
        source = lag + col == s
        from_col = (lk >= 0) & ((lk < 4) | (y < 3))
        from_row = (k >= 0) & (col >= k)
        sent_all(col_children(lk_at), xcol.at[lk_at], col_send.at[lk_at], from_col)
        sent_all(row_children(k_at), xrow.at[k_at], row_send.at[k_at], from_row)
        return carry

    lax.fori_loop(0, STEPS, drain, 0)


def per_device(right_side, upper_left, upper_right, vectors_left, vectors_right, values_left, values_right):
    size = right_side.shape[0]
    tile = pltpu.VMEM((size, size), BF16)
    tiles = pltpu.VMEM((STEPS, size, size), BF16)
    sems = pltpu.SemaphoreType.DMA
    vmem = pl.BlockSpec(memory_space=pltpu.VMEM)
    return pl.pallas_call(
        kernel,
        out_shape=jax.ShapeDtypeStruct((size, size), F32),
        in_specs=[pl.BlockSpec(memory_space=pl.ANY)] * 7,
        out_specs=vmem,
        scratch_shapes=[
            tile, tile, pltpu.VMEM((1, size), F32), pltpu.VMEM((1, size), F32),
            tile, tile, pltpu.VMEM((size, size), F32), tile, tile, tile,
            tiles, tiles, tiles, tiles,
            sems((STEPS, CHUNKS)), sems((STEPS, CHUNKS)), sems((STEPS, CHUNKS)), sems((STEPS, CHUNKS)),
            sems((STEPS, 5)), sems((STEPS, 2)), sems((STEPS, 2)), sems((STEPS, 4)),
            sems((CHUNKS,)), sems((5,)),
            pltpu.SemaphoreType.REGULAR,
        ],
        compiler_params=pltpu.CompilerParams(
            collective_id=0, has_side_effects=True, vmem_limit_bytes=48 << 20
        ),
        name="sylvester",
    )(
        right_side, upper_left, upper_right, vectors_left, vectors_right,
        values_left.reshape(1, size), values_right.reshape(1, size),
    )


def solution(mesh):
    in_specs = (
        P("row", "col"),
        P("row", "col"),
        P("row", "col"),
        P("row", None),
        P("col", None),
        P("row"),
        P("col"),
    )
    return jax.shard_map(
        per_device, mesh=mesh, in_specs=in_specs, out_specs=P("row", "col"), check_vma=False
    )
```

```python
import jax
import jax.numpy as jnp
from jax import lax
from jax.experimental import pallas as pl
from jax.experimental.pallas import tpu as pltpu
from jax.sharding import PartitionSpec as P

STEPS = 8
SIDE = 16
CHUNKS = 4
MESH = pl.DeviceIdType.MESH
BF16 = jnp.bfloat16
F32 = jnp.float32


def column_edges():
    edges = set()
    for chip in range(8):
        edges.add((2 * chip, 2 * chip + 1))
        if chip < 7:
            edges.add((2 * chip, 2 * chip + 2))
            edges.add((2 * chip + 1, 2 * chip + 2))
    edges |= {(0, far) for far in range(10, 16)}
    edges |= {(2, far) for far in range(8, 10)}
    edges |= {(0, 2)}
    edges |= {(far - 1, far) for far in range(9, 16)}
    return edges


def dot(left, right):
    return jnp.dot(left, right, preferred_element_type=F32)


def kernel(
    c_any, a_any, b_any, u_any, v_any, al_any, bl_any, o_ref,
    u_ref, v_ref, al_ref, bl_ref,
    ut, vt, inv, hbuf, ybuf, solved, xcol, xrow, abuf, bbuf,
    col_recv, row_recv, a_recv, b_recv,
    col_send, row_send, a_send, b_send, a_first, loaded, token,
):
    row = lax.axis_index("row")
    col = lax.axis_index("col")
    lag = SIDE - 1 - row
    x = row % 4
    y = row // 4
    even = col % 2 == 0
    size = o_ref.shape[0]
    part = size // CHUNKS
    parts = [pl.ds(p * part, part) for p in range(CHUNKS)]

    def row_of(x_to, y_to):
        return ((y_to + 4) % 4) * 4 + (x_to + 4) % 4

    x_minus, x_plus = row_of(x - 1, y), row_of(x + 1, y)
    y_minus, y_plus = row_of(x, y - 1), row_of(x, y + 1)

    def copy(src, dst, send, recv, to_row, to_col):
        return pltpu.make_async_remote_copy(
            src_ref=src, dst_ref=dst, send_sem=send, recv_sem=recv,
            device_id=(to_row, to_col), device_id_type=MESH,
        )

    def received(dst, recv):
        copy(dst, dst, recv, recv, row, col).wait_recv()

    loads = [
        pltpu.make_async_copy(src, dst, loaded.at[index])
        for index, (src, dst) in enumerate(
            [(c_any, o_ref), (u_any, u_ref), (v_any, v_ref), (al_any, al_ref), (bl_any, bl_ref)]
        )
    ]
    for load in loads:
        load.start()

    barrier = pltpu.get_barrier_semaphore()
    for near in (x_minus, x_plus, y_minus, y_plus):
        pl.semaphore_signal(barrier, inc=1, device_id=(near, col), device_id_type=MESH)
    for mine, other in ((12, 11), (11, 12)):
        @pl.when(row == mine)
        def _():
            pl.semaphore_signal(barrier, inc=1, device_id=(other, col), device_id_type=MESH)
    count = 4 + ((row == 11) | (row == 12)).astype(jnp.int32)
    edges = column_edges()
    for other in range(SIDE):
        near = sorted({b for a, b in edges if a == other} | {a for a, b in edges if b == other})
        hit = col == near[0]
        for mine in near[1:]:
            hit = hit | (col == mine)

        @pl.when(hit)
        def _():
            pl.semaphore_signal(barrier, inc=1, device_id=(row, other), device_id_type=MESH)

        count = count + hit.astype(jnp.int32)
    pl.semaphore_wait(barrier, count)

    def a_children(t):
        mine = lag > t
        last = STEPS - 1 - t
        onward = even & (t < 6) & (col + 2 <= last)
        back = (t >= 6) & (col == 2)
        side = even & (col + 1 <= last)
        return [
            (mine & (onward | back), row, jnp.where(onward, col + 2, 0)),
            (mine & side, row, jnp.minimum(col + 1, SIDE - 1)),
        ]

    def a_receives(t):
        return (lag > t) & ((col <= STEPS - 1 - t) | ((t >= 6) & (col == 2)))

    def b_children(k):
        xs = k % 4
        low = k < 4
        high = ~low
        right = x >= xs
        d = (xs - x + 4) % 4
        up, down = high & (k % 2 == 0), high & (k % 2 == 1)
        mine = col > k
        return [
            (mine & ((low & (y == 0)) | (down & right & ((y == 1) | (y == 0)))), y_minus, col),
            (
                mine & right & ((low & ((y == 0) | (y == 1))) | (up & ((y == 1) | (y == 2)))),
                y_plus, col,
            ),
            (mine & low & (y == 0) & (d == 0), x_minus, col),
            (
                mine & ((low & (y == 0) & ((d == 0) | (d == 3))) | (high & (y == 1) & right & (x < 3))),
                x_plus, col,
            ),
        ]

    def b_receives(k):
        right = x >= k % 4
        low = k < 4
        across = jnp.where(k % 2 == 0, 2, 0)
        return (col > k) & (row != k) & (
            (low & ((y == 3) | (y == 0) | right))
            | ((~low) & right & ((y == 1) | (y == 3) | (y == across)))
        )

    def col_children(lk):
        rk = SIDE - 1 - lk
        xk, yk = rk % 4, rk // 4
        d = (xk - x + 4) % 4
        own = y == yk
        return [
            (own & (d == 0), x_minus, col),
            (own & (d == 0) & (lk == 3), row_of(3, 2), col),
            (own & ((d == 0) | (d == 3)), x_plus, col),
            (
                (own & (yk == 3) & ((lk != 3) | (x != 3))) | ((yk == 2) & ((y == 2) | (y == 1))),
                y_minus, col,
            ),
            ((yk == 3) & ((y == 3) | (y == 0)), y_plus, col),
        ]

    def row_children(k):
        return [
            (even & (col < SIDE - 1), row, jnp.minimum(col + 1, SIDE - 1)),
            ((col < SIDE - 2) & (even | (col == k)), row, jnp.minimum((col // 2 + 1) * 2, SIDE - 1)),
        ]

    def send_all(children, src, dst, sends, recv, where=True):
        for index, (condition, to_row, to_col) in enumerate(children):
            @pl.when(condition & where)
            def _():
                copy(src, dst, sends.at[index], recv, to_row, to_col).start()

    def sent_all(children, whole, sends, where=True):
        for index, (condition, to_row, to_col) in enumerate(children):
            @pl.when(condition & where)
            def _():
                copy(whole, whole, sends.at[index], sends.at[index], row, col).wait_send()

    is_b_source = (row < STEPS) & (col > row)
    b_own = jnp.minimum(row, STEPS - 1)
    for p, rows in enumerate(parts):
        send_all(
            b_children(b_own), b_any.at[rows], bbuf.at[b_own, rows], b_send.at[b_own],
            b_recv.at[b_own, p], is_b_source,
        )

    t_own = jnp.minimum(SIDE - 1 - col, STEPS - 1)
    is_a_source = (col >= SIDE - STEPS) & (lag > t_own)
    a_target = jnp.where(t_own < 6, 0, 2)
    a_copies = [
        copy(
            a_any.at[rows], abuf.at[t_own, rows], a_first.at[p], a_recv.at[t_own, p], row, a_target
        )
        for p, rows in enumerate(parts)
    ]

    @pl.when(is_a_source & (t_own != 0) & (t_own != 6))
    def _():
        pl.semaphore_wait(token, 1)

    @pl.when(is_a_source)
    def _():
        for this in a_copies:
            this.start()
        for this in a_copies[:-1]:
            this.wait_send()

    @pl.when(is_a_source & (t_own != 5) & (t_own != 7) & (lag > t_own + 1))
    def _():
        pl.semaphore_signal(token, inc=1, device_id=(row, col - 1), device_id_type=MESH)

    for load in loads:
        load.wait()
    ut[...] = u_ref[...].astype(F32).T.astype(BF16)
    vt[...] = v_ref[...].astype(F32).T.astype(BF16)
    sums = jnp.broadcast_to(al_ref[...], (size, size)).T + jnp.broadcast_to(bl_ref[...], (size, size))
    inv[...] = 1.0 / sums

    def relay(condition, children, buffer, recvs, sends):
        @pl.when(condition)
        def _():
            for p, rows in enumerate(parts):
                tile = buffer.at[rows]
                received(tile, recvs.at[p])
                send_all(children, tile, tile, sends, recvs.at[p])

    def take_b(q, carry):
        near = jnp.where(q % 3 == 0, 1, jnp.where(q % 3 == 1, 3, 2))
        source_row = jnp.where(q < 3, (x + near) % 4, jnp.where(q == 3, 5, 7))
        high = x + 3 - q
        turn = jnp.where(q == 3, 0, jnp.where(q == 4, 1, jnp.where(q == 5, 3, 2)))
        k = jnp.where(
            y == 0, source_row,
            jnp.where(y == 1, jnp.where(q < 3, high, (x + turn) % 4), 4 + 2 * q),
        )
        valid = jnp.where(
            y == 0, q < 5, jnp.where(y == 1, ((q >= 3) | (high >= 4)) & (q < 7), (y == 2) & (q < 2))
        )
        at = jnp.clip(k, 0, STEPS - 1)
        relay(valid & b_receives(at), b_children(at), bbuf.at[at], b_recv.at[at], b_send.at[at])
        return carry

    @pl.when((y < 3) & (col > 0))
    def _():
        lax.fori_loop(0, STEPS - 1, take_b, 0)

    def step(s, carry):
        @pl.when(even & (col < STEPS) & (s < 4))
        def _():
            first = jnp.where(s < 2, 2 * s, jnp.where(s == 2, 4, 5))
            second = jnp.minimum(jnp.where(s < 2, 2 * s + 1, s + 4), STEPS - 1)
            for t in (first, second):
                relay(a_receives(t), a_children(t), abuf.at[t], a_recv.at[t], a_send.at[t])

        lk = s - col
        k = s - lag
        lk_at, k_at = jnp.maximum(lk, 0), jnp.maximum(k, 0)
        mine = lag + col == s
        from_col = (lk >= 0) & (lag != lk) & ((lk < 4) | (y < 3))
        from_row = (k >= 0) & (col > k)
        use_col = (lk >= 0) & (lag > lk)

        to_col, to_row = col_children(lk_at), row_children(k_at)

        @pl.when(mine)
        def _():
            rounded = o_ref[...].astype(BF16)
            hbuf[...] = dot(ut[...], rounded).astype(BF16)
            ybuf[...] = (dot(hbuf[...], v_ref[...]) * inv[...]).astype(BF16)
            for p, rows in enumerate(parts):
                turned = dot(u_ref[rows, :], ybuf[...]).astype(BF16)
                answer = dot(turned, vt[...])
                o_ref[rows, :] = answer
                solved[rows, :] = answer.astype(BF16)
                src = solved.at[rows]
                send_all(
                    to_col, src, xcol.at[lk_at, rows], col_send.at[lk_at], col_recv.at[lk_at, p]
                )
                send_all(
                    to_row, src, xrow.at[k_at, rows], row_send.at[k_at], row_recv.at[k_at, p]
                )

        relay(from_row, to_row, xrow.at[k_at], row_recv.at[k_at], row_send.at[k_at])

        @pl.when(from_row)
        def _():
            for p, rows in enumerate(parts):
                received(bbuf.at[k_at, rows], b_recv.at[k_at, p])
            for p, rows in enumerate(parts):
                o_ref[rows, :] -= dot(xrow[k_at, rows, :], bbuf[k_at])

        @pl.when(use_col & ~even)
        def _():
            for p, rows in enumerate(parts):
                received(abuf.at[lk_at, rows], a_recv.at[lk_at, p])

        @pl.when(from_col)
        def _():
            for p, rows in enumerate(parts):
                tile = xcol.at[lk_at, rows]
                received(tile, col_recv.at[lk_at, p])
                send_all(to_col, tile, tile, col_send.at[lk_at], col_recv.at[lk_at, p])

                @pl.when(use_col)
                def _():
                    o_ref[...] -= dot(abuf[lk_at, :, rows], xcol[lk_at, rows, :])

        return carry

    lax.fori_loop(0, STEPS, step, 0)

    sent_all(b_children(b_own), bbuf.at[b_own], b_send.at[b_own], is_b_source)

    @pl.when(is_a_source)
    def _():
        a_copies[-1].wait_send()

    def drain(s, carry):
        sent_all(a_children(s), abuf.at[s], a_send.at[s], a_receives(s))
        sent_all(b_children(s), bbuf.at[s], b_send.at[s], b_receives(s))
        lk = s - col
        k = s - lag
        lk_at, k_at = jnp.maximum(lk, 0), jnp.maximum(k, 0)
        source = lag + col == s
        from_col = (lk >= 0) & ((lk < 4) | (y < 3))
        from_row = (k >= 0) & (col >= k)
        sent_all(col_children(lk_at), xcol.at[lk_at], col_send.at[lk_at], from_col)
        sent_all(row_children(k_at), xrow.at[k_at], row_send.at[k_at], from_row)
        return carry

    lax.fori_loop(0, STEPS, drain, 0)


def per_device(right_side, upper_left, upper_right, vectors_left, vectors_right, values_left, values_right):
    size = right_side.shape[0]
    tile = pltpu.VMEM((size, size), BF16)
    tiles = pltpu.VMEM((STEPS, size, size), BF16)
    sems = pltpu.SemaphoreType.DMA
    vmem = pl.BlockSpec(memory_space=pltpu.VMEM)
    return pl.pallas_call(
        kernel,
        out_shape=jax.ShapeDtypeStruct((size, size), F32),
        in_specs=[pl.BlockSpec(memory_space=pl.ANY)] * 7,
        out_specs=vmem,
        scratch_shapes=[
            tile, tile, pltpu.VMEM((1, size), F32), pltpu.VMEM((1, size), F32),
            tile, tile, pltpu.VMEM((size, size), F32), tile, tile, tile,
            tiles, tiles, tiles, tiles,
            sems((STEPS, CHUNKS)), sems((STEPS, CHUNKS)), sems((STEPS, CHUNKS)), sems((STEPS, CHUNKS)),
            sems((STEPS, 5)), sems((STEPS, 2)), sems((STEPS, 2)), sems((STEPS, 4)),
            sems((CHUNKS,)), sems((5,)),
            pltpu.SemaphoreType.REGULAR,
        ],
        compiler_params=pltpu.CompilerParams(
            collective_id=0, has_side_effects=True, vmem_limit_bytes=48 << 20
        ),
        name="sylvester",
    )(
        right_side, upper_left, upper_right, vectors_left, vectors_right,
        values_left.reshape(1, size), values_right.reshape(1, size),
    )


def solution(mesh):
    in_specs = (
        P("row", "col"),
        P("row", "col"),
        P("row", "col"),
        P("row", None),
        P("col", None),
        P("row"),
        P("col"),
    )
    return jax.shard_map(
        per_device, mesh=mesh, in_specs=in_specs, out_specs=P("row", "col"), check_vma=False
    )
```

```python
import jax
import jax.numpy as jnp
from jax import lax
from jax.experimental import pallas as pl
from jax.experimental.pallas import tpu as pltpu
from jax.sharding import PartitionSpec as P

STEPS = 8
SIDE = 16
CHUNKS = 8
MESH = pl.DeviceIdType.MESH
BF16 = jnp.bfloat16
F32 = jnp.float32


def column_edges():
    edges = set()
    for chip in range(8):
        edges.add((2 * chip, 2 * chip + 1))
        if chip < 7:
            edges.add((2 * chip, 2 * chip + 2))
            edges.add((2 * chip + 1, 2 * chip + 2))
    edges |= {(0, far) for far in range(10, 16)}
    edges |= {(2, far) for far in range(8, 10)}
    edges |= {(0, 2)}
    edges |= {(far - 1, far) for far in range(9, 16)}
    return edges


def dot(left, right):
    return jnp.dot(left, right, preferred_element_type=F32)


def kernel(
    c_any, a_any, b_any, u_any, v_any, al_any, bl_any, o_ref,
    u_ref, v_ref, al_ref, bl_ref,
    ut, vt, inv, hbuf, ybuf, solved, xcol, xrow, abuf, bbuf,
    col_recv, row_recv, a_recv, b_recv,
    col_send, row_send, a_send, b_send, a_first, loaded, token,
):
    row = lax.axis_index("row")
    col = lax.axis_index("col")
    lag = SIDE - 1 - row
    x = row % 4
    y = row // 4
    even = col % 2 == 0
    size = o_ref.shape[0]
    part = size // CHUNKS
    parts = [pl.ds(p * part, part) for p in range(CHUNKS)]

    def row_of(x_to, y_to):
        return ((y_to + 4) % 4) * 4 + (x_to + 4) % 4

    x_minus, x_plus = row_of(x - 1, y), row_of(x + 1, y)
    y_minus, y_plus = row_of(x, y - 1), row_of(x, y + 1)

    def copy(src, dst, send, recv, to_row, to_col):
        return pltpu.make_async_remote_copy(
            src_ref=src, dst_ref=dst, send_sem=send, recv_sem=recv,
            device_id=(to_row, to_col), device_id_type=MESH,
        )

    def received(dst, recv):
        copy(dst, dst, recv, recv, row, col).wait_recv()

    loads = [
        pltpu.make_async_copy(src, dst, loaded.at[index])
        for index, (src, dst) in enumerate(
            [(c_any, o_ref), (u_any, u_ref), (v_any, v_ref), (al_any, al_ref), (bl_any, bl_ref)]
        )
    ]
    for load in loads:
        load.start()

    barrier = pltpu.get_barrier_semaphore()
    for near in (x_minus, x_plus, y_minus, y_plus):
        pl.semaphore_signal(barrier, inc=1, device_id=(near, col), device_id_type=MESH)
    for mine, other in ((12, 11), (11, 12)):
        @pl.when(row == mine)
        def _():
            pl.semaphore_signal(barrier, inc=1, device_id=(other, col), device_id_type=MESH)
    count = 4 + ((row == 11) | (row == 12)).astype(jnp.int32)
    edges = column_edges()
    for other in range(SIDE):
        near = sorted({b for a, b in edges if a == other} | {a for a, b in edges if b == other})
        hit = col == near[0]
        for mine in near[1:]:
            hit = hit | (col == mine)

        @pl.when(hit)
        def _():
            pl.semaphore_signal(barrier, inc=1, device_id=(row, other), device_id_type=MESH)

        count = count + hit.astype(jnp.int32)
    for load in loads:
        load.wait()
    ut[...] = u_ref[...].astype(F32).T.astype(BF16)
    vt[...] = v_ref[...].astype(F32).T.astype(BF16)
    sums = jnp.broadcast_to(al_ref[...], (size, size)).T + jnp.broadcast_to(bl_ref[...], (size, size))
    inv[...] = 1.0 / sums

    pl.semaphore_wait(barrier, count)

    def a_children(t):
        mine = lag > t
        last = STEPS - 1 - t
        onward = even & (t < 6) & (col + 2 <= last)
        back = (t >= 6) & (col == 2)
        side = even & (col + 1 <= last)
        return [
            (mine & (onward | back), row, jnp.where(onward, col + 2, 0)),
            (mine & side, row, jnp.minimum(col + 1, SIDE - 1)),
        ]

    def a_receives(t):
        return (lag > t) & ((col <= STEPS - 1 - t) | ((t >= 6) & (col == 2)))

    def b_children(k):
        xs = k % 4
        low = k < 4
        high = ~low
        right = x >= xs
        d = (xs - x + 4) % 4
        up, down = high & (k % 2 == 0), high & (k % 2 == 1)
        mine = col > k
        return [
            (mine & ((low & (y == 0)) | (down & right & ((y == 1) | (y == 0)))), y_minus, col),
            (
                mine & right & ((low & ((y == 0) | (y == 1))) | (up & ((y == 1) | (y == 2)))),
                y_plus, col,
            ),
            (mine & low & (y == 0) & (d == 0), x_minus, col),
            (
                mine & ((low & (y == 0) & ((d == 0) | (d == 3))) | (high & (y == 1) & right & (x < 3))),
                x_plus, col,
            ),
        ]

    def b_receives(k):
        right = x >= k % 4
        low = k < 4
        across = jnp.where(k % 2 == 0, 2, 0)
        return (col > k) & (row != k) & (
            (low & ((y == 3) | (y == 0) | right))
            | ((~low) & right & ((y == 1) | (y == 3) | (y == across)))
        )

    def col_children(lk):
        rk = SIDE - 1 - lk
        xk, yk = rk % 4, rk // 4
        d = (xk - x + 4) % 4
        own = y == yk
        return [
            (own & (d == 0), x_minus, col),
            (own & (d == 0) & (lk == 3), row_of(3, 2), col),
            (own & ((d == 0) | (d == 3)), x_plus, col),
            (
                (own & (yk == 3) & ((lk != 3) | (x != 3))) | ((yk == 2) & ((y == 2) | (y == 1))),
                y_minus, col,
            ),
            ((yk == 3) & ((y == 3) | (y == 0)), y_plus, col),
        ]

    def row_children(k):
        return [
            (even & (col < SIDE - 1), row, jnp.minimum(col + 1, SIDE - 1)),
            ((col < SIDE - 2) & (even | (col == k)), row, jnp.minimum((col // 2 + 1) * 2, SIDE - 1)),
        ]

    def send_all(children, src, dst, sends, recv, where=True):
        for index, (condition, to_row, to_col) in enumerate(children):
            @pl.when(condition & where)
            def _():
                copy(src, dst, sends.at[index], recv, to_row, to_col).start()

    def sent_all(children, whole, sends, where=True):
        for index, (condition, to_row, to_col) in enumerate(children):
            @pl.when(condition & where)
            def _():
                copy(whole, whole, sends.at[index], sends.at[index], row, col).wait_send()

    is_b_source = (row < STEPS) & (col > row)
    b_own = jnp.minimum(row, STEPS - 1)
    for p, rows in enumerate(parts):
        send_all(
            b_children(b_own), b_any.at[rows], bbuf.at[b_own, rows], b_send.at[b_own],
            b_recv.at[b_own, p], is_b_source,
        )

    t_own = jnp.minimum(SIDE - 1 - col, STEPS - 1)
    is_a_source = (col >= SIDE - STEPS) & (lag > t_own)
    a_target = jnp.where(t_own < 6, 0, 2)
    a_copies = [
        copy(
            a_any.at[rows], abuf.at[t_own, rows], a_first.at[p], a_recv.at[t_own, p], row, a_target
        )
        for p, rows in enumerate(parts)
    ]

    @pl.when(is_a_source & (t_own != 0) & (t_own != 6))
    def _():
        pl.semaphore_wait(token, 1)

    @pl.when(is_a_source)
    def _():
        for this in a_copies:
            this.start()
        for this in a_copies[:-1]:
            this.wait_send()

    @pl.when(is_a_source & (t_own != 5) & (t_own != 7) & (lag > t_own + 1))
    def _():
        pl.semaphore_signal(token, inc=1, device_id=(row, col - 1), device_id_type=MESH)

    def relay(condition, children, buffer, recvs, sends):
        @pl.when(condition)
        def _():
            for p, rows in enumerate(parts):
                tile = buffer.at[rows]
                received(tile, recvs.at[p])
                send_all(children, tile, tile, sends, recvs.at[p])

    def take_b(q, carry):
        near = jnp.where(q % 3 == 0, 1, jnp.where(q % 3 == 1, 3, 2))
        source_row = jnp.where(q < 3, (x + near) % 4, jnp.where(q == 3, 5, 7))
        high = x + 3 - q
        turn = jnp.where(q == 3, 0, jnp.where(q == 4, 1, jnp.where(q == 5, 3, 2)))
        k = jnp.where(
            y == 0, source_row,
            jnp.where(y == 1, jnp.where(q < 3, high, (x + turn) % 4), 4 + 2 * q),
        )
        valid = jnp.where(
            y == 0, q < 5, jnp.where(y == 1, ((q >= 3) | (high >= 4)) & (q < 7), (y == 2) & (q < 2))
        )
        at = jnp.clip(k, 0, STEPS - 1)
        relay(valid & b_receives(at), b_children(at), bbuf.at[at], b_recv.at[at], b_send.at[at])
        return carry

    @pl.when((y < 3) & (col > 0))
    def _():
        lax.fori_loop(0, STEPS - 1, take_b, 0)

    def step(s, carry):
        @pl.when(even & (col < STEPS) & (s < 4))
        def _():
            first = jnp.where(s < 2, 2 * s, jnp.where(s == 2, 4, 5))
            second = jnp.minimum(jnp.where(s < 2, 2 * s + 1, s + 4), STEPS - 1)
            for t in (first, second):
                relay(a_receives(t), a_children(t), abuf.at[t], a_recv.at[t], a_send.at[t])

        lk = s - col
        k = s - lag
        lk_at, k_at = jnp.maximum(lk, 0), jnp.maximum(k, 0)
        mine = lag + col == s
        from_col = (lk >= 0) & (lag != lk) & ((lk < 4) | (y < 3))
        from_row = (k >= 0) & (col > k)
        use_col = (lk >= 0) & (lag > lk)

        to_col, to_row = col_children(lk_at), row_children(k_at)

        @pl.when(mine)
        def _():
            rounded = o_ref[...].astype(BF16)
            hbuf[...] = dot(ut[...], rounded).astype(BF16)
            ybuf[...] = (dot(hbuf[...], v_ref[...]) * inv[...]).astype(BF16)
            for p, rows in enumerate(parts):
                turned = dot(u_ref[rows, :], ybuf[...]).astype(BF16)
                answer = dot(turned, vt[...])
                o_ref[rows, :] = answer
                solved[rows, :] = answer.astype(BF16)
                src = solved.at[rows]
                send_all(
                    to_col, src, xcol.at[lk_at, rows], col_send.at[lk_at], col_recv.at[lk_at, p]
                )
                send_all(
                    to_row, src, xrow.at[k_at, rows], row_send.at[k_at], row_recv.at[k_at, p]
                )

        relay(from_row, to_row, xrow.at[k_at], row_recv.at[k_at], row_send.at[k_at])

        @pl.when(from_row)
        def _():
            for p, rows in enumerate(parts):
                received(bbuf.at[k_at, rows], b_recv.at[k_at, p])
            for p, rows in enumerate(parts):
                o_ref[rows, :] -= dot(xrow[k_at, rows, :], bbuf[k_at])

        @pl.when(use_col & ~even)
        def _():
            for p, rows in enumerate(parts):
                received(abuf.at[lk_at, rows], a_recv.at[lk_at, p])

        @pl.when(from_col)
        def _():
            for p, rows in enumerate(parts):
                tile = xcol.at[lk_at, rows]
                received(tile, col_recv.at[lk_at, p])
                send_all(to_col, tile, tile, col_send.at[lk_at], col_recv.at[lk_at, p])

                @pl.when(use_col)
                def _():
                    o_ref[...] -= dot(abuf[lk_at, :, rows], xcol[lk_at, rows, :])

        return carry

    lax.fori_loop(0, STEPS, step, 0)

    sent_all(b_children(b_own), bbuf.at[b_own], b_send.at[b_own], is_b_source)

    @pl.when(is_a_source)
    def _():
        a_copies[-1].wait_send()

    def drain(s, carry):
        sent_all(a_children(s), abuf.at[s], a_send.at[s], a_receives(s))
        sent_all(b_children(s), bbuf.at[s], b_send.at[s], b_receives(s))
        lk = s - col
        k = s - lag
        lk_at, k_at = jnp.maximum(lk, 0), jnp.maximum(k, 0)
        source = lag + col == s
        from_col = (lk >= 0) & ((lk < 4) | (y < 3))
        from_row = (k >= 0) & (col >= k)
        sent_all(col_children(lk_at), xcol.at[lk_at], col_send.at[lk_at], from_col)
        sent_all(row_children(k_at), xrow.at[k_at], row_send.at[k_at], from_row)
        return carry

    lax.fori_loop(0, STEPS, drain, 0)


def per_device(right_side, upper_left, upper_right, vectors_left, vectors_right, values_left, values_right):
    size = right_side.shape[0]
    tile = pltpu.VMEM((size, size), BF16)
    tiles = pltpu.VMEM((STEPS, size, size), BF16)
    sems = pltpu.SemaphoreType.DMA
    vmem = pl.BlockSpec(memory_space=pltpu.VMEM)
    return pl.pallas_call(
        kernel,
        out_shape=jax.ShapeDtypeStruct((size, size), F32),
        in_specs=[pl.BlockSpec(memory_space=pl.ANY)] * 7,
        out_specs=vmem,
        scratch_shapes=[
            tile, tile, pltpu.VMEM((1, size), F32), pltpu.VMEM((1, size), F32),
            tile, tile, pltpu.VMEM((size, size), F32), tile, tile, tile,
            tiles, tiles, tiles, tiles,
            sems((STEPS, CHUNKS)), sems((STEPS, CHUNKS)), sems((STEPS, CHUNKS)), sems((STEPS, CHUNKS)),
            sems((STEPS, 5)), sems((STEPS, 2)), sems((STEPS, 2)), sems((STEPS, 4)),
            sems((CHUNKS,)), sems((5,)),
            pltpu.SemaphoreType.REGULAR,
        ],
        compiler_params=pltpu.CompilerParams(
            collective_id=0, has_side_effects=True, vmem_limit_bytes=67043328
        ),
        name="sylvester",
    )(
        right_side, upper_left, upper_right, vectors_left, vectors_right,
        values_left.reshape(1, size), values_right.reshape(1, size),
    )


def solution(mesh):
    in_specs = (
        P("row", "col"),
        P("row", "col"),
        P("row", "col"),
        P("row", None),
        P("col", None),
        P("row"),
        P("col"),
    )
    return jax.shard_map(
        per_device, mesh=mesh, in_specs=in_specs, out_specs=P("row", "col"), check_vma=False
    )
```

```python
import jax
import jax.numpy as jnp
from jax import lax
from jax.experimental import pallas as pl
from jax.experimental.pallas import tpu as pltpu
from jax.sharding import PartitionSpec as P

STEPS = 8
SIDE = 16
CHUNKS = 8
MESH = pl.DeviceIdType.MESH
BF16 = jnp.bfloat16
F32 = jnp.float32


def column_edges():
    edges = set()
    for chip in range(8):
        edges.add((2 * chip, 2 * chip + 1))
        if chip < 7:
            edges.add((2 * chip, 2 * chip + 2))
            edges.add((2 * chip + 1, 2 * chip + 2))
    edges |= {(0, far) for far in range(10, 16)}
    edges |= {(2, far) for far in range(8, 10)}
    edges |= {(0, 2)}
    edges |= {(far - 1, far) for far in range(9, 16)}
    return edges


def dot(left, right):
    return jnp.dot(left, right, preferred_element_type=F32)


def kernel(
    c_any, a_any, b_any, u_any, v_any, al_any, bl_any, o_ref,
    u_ref, v_ref, al_ref, bl_ref,
    ut, vt, inv, hbuf, ybuf, solved, xcol, xrow, abuf, bbuf,
    col_recv, row_recv, a_recv, b_recv,
    col_send, row_send, a_send, b_send, a_first, loaded, token,
):
    row = lax.axis_index("row")
    col = lax.axis_index("col")
    lag = SIDE - 1 - row
    x = row % 4
    y = row // 4
    even = col % 2 == 0
    size = o_ref.shape[0]
    part = size // CHUNKS
    parts = [pl.ds(p * part, part) for p in range(CHUNKS)]
    large = [pl.ds(2 * p * part, 2 * part) for p in range(CHUNKS // 2)]

    def row_of(x_to, y_to):
        return ((y_to + 4) % 4) * 4 + (x_to + 4) % 4

    x_minus, x_plus = row_of(x - 1, y), row_of(x + 1, y)
    y_minus, y_plus = row_of(x, y - 1), row_of(x, y + 1)

    def copy(src, dst, send, recv, to_row, to_col):
        return pltpu.make_async_remote_copy(
            src_ref=src, dst_ref=dst, send_sem=send, recv_sem=recv,
            device_id=(to_row, to_col), device_id_type=MESH,
        )

    def received(dst, recv):
        copy(dst, dst, recv, recv, row, col).wait_recv()

    loads = [
        pltpu.make_async_copy(src, dst, loaded.at[index])
        for index, (src, dst) in enumerate(
            [(c_any, o_ref), (u_any, u_ref), (v_any, v_ref), (al_any, al_ref), (bl_any, bl_ref)]
        )
    ]
    for load in loads:
        load.start()

    barrier = pltpu.get_barrier_semaphore()
    for near in (x_minus, x_plus, y_minus, y_plus):
        pl.semaphore_signal(barrier, inc=1, device_id=(near, col), device_id_type=MESH)
    for mine, other in ((12, 11), (11, 12)):
        @pl.when(row == mine)
        def _():
            pl.semaphore_signal(barrier, inc=1, device_id=(other, col), device_id_type=MESH)
    count = 4 + ((row == 11) | (row == 12)).astype(jnp.int32)
    edges = column_edges()
    for other in range(SIDE):
        near = sorted({b for a, b in edges if a == other} | {a for a, b in edges if b == other})
        hit = col == near[0]
        for mine in near[1:]:
            hit = hit | (col == mine)

        @pl.when(hit)
        def _():
            pl.semaphore_signal(barrier, inc=1, device_id=(row, other), device_id_type=MESH)

        count = count + hit.astype(jnp.int32)
    for load in loads:
        load.wait()
    ut[...] = u_ref[...].astype(F32).T.astype(BF16)
    vt[...] = v_ref[...].astype(F32).T.astype(BF16)
    sums = jnp.broadcast_to(al_ref[...], (size, size)).T + jnp.broadcast_to(bl_ref[...], (size, size))
    inv[...] = 1.0 / sums

    pl.semaphore_wait(barrier, count)

    def a_children(t):
        mine = lag > t
        last = STEPS - 1 - t
        onward = even & (t < 6) & (col + 2 <= last)
        back = (t >= 6) & (col == 2)
        side = even & (col + 1 <= last)
        return [
            (mine & (onward | back), row, jnp.where(onward, col + 2, 0)),
            (mine & side, row, jnp.minimum(col + 1, SIDE - 1)),
        ]

    def a_receives(t):
        return (lag > t) & ((col <= STEPS - 1 - t) | ((t >= 6) & (col == 2)))

    def b_children(k):
        xs = k % 4
        low = k < 4
        high = ~low
        right = x >= xs
        d = (xs - x + 4) % 4
        up, down = high & (k % 2 == 0), high & (k % 2 == 1)
        mine = col > k
        return [
            (mine & ((low & (y == 0)) | (down & right & ((y == 1) | (y == 0)))), y_minus, col),
            (
                mine & right & ((low & ((y == 0) | (y == 1))) | (up & ((y == 1) | (y == 2)))),
                y_plus, col,
            ),
            (mine & low & (y == 0) & (d == 0), x_minus, col),
            (
                mine & ((low & (y == 0) & ((d == 0) | (d == 3))) | (high & (y == 1) & right & (x < 3))),
                x_plus, col,
            ),
        ]

    def b_receives(k):
        right = x >= k % 4
        low = k < 4
        across = jnp.where(k % 2 == 0, 2, 0)
        return (col > k) & (row != k) & (
            (low & ((y == 3) | (y == 0) | right))
            | ((~low) & right & ((y == 1) | (y == 3) | (y == across)))
        )

    def col_children(lk):
        rk = SIDE - 1 - lk
        xk, yk = rk % 4, rk // 4
        d = (xk - x + 4) % 4
        own = y == yk
        return [
            (own & (d == 0), x_minus, col),
            (own & (d == 0) & (lk == 3), row_of(3, 2), col),
            (own & ((d == 0) | (d == 3)), x_plus, col),
            (
                (own & (yk == 3) & ((lk != 3) | (x != 3))) | ((yk == 2) & ((y == 2) | (y == 1))),
                y_minus, col,
            ),
            ((yk == 3) & ((y == 3) | (y == 0)), y_plus, col),
        ]

    def row_children(k):
        return [
            (even & (col < SIDE - 1), row, jnp.minimum(col + 1, SIDE - 1)),
            ((col < SIDE - 2) & (even | (col == k)), row, jnp.minimum((col // 2 + 1) * 2, SIDE - 1)),
        ]

    def send_all(children, src, dst, sends, recv, where=True):
        for index, (condition, to_row, to_col) in enumerate(children):
            @pl.when(condition & where)
            def _():
                copy(src, dst, sends.at[index], recv, to_row, to_col).start()

    def sent_all(children, whole, sends, where=True):
        for index, (condition, to_row, to_col) in enumerate(children):
            @pl.when(condition & where)
            def _():
                copy(whole, whole, sends.at[index], sends.at[index], row, col).wait_send()

    is_b_source = (row < STEPS) & (col > row)
    b_own = jnp.minimum(row, STEPS - 1)
    for p, rows in enumerate(large):
        send_all(
            b_children(b_own), b_any.at[rows], bbuf.at[b_own, rows], b_send.at[b_own],
            b_recv.at[b_own, p], is_b_source,
        )

    t_own = jnp.minimum(SIDE - 1 - col, STEPS - 1)
    is_a_source = (col >= SIDE - STEPS) & (lag > t_own)
    a_target = jnp.where(t_own < 6, 0, 2)
    a_copies = [
        copy(
            a_any.at[rows], abuf.at[t_own, rows], a_first.at[p], a_recv.at[t_own, p], row, a_target
        )
        for p, rows in enumerate(large)
    ]

    @pl.when(is_a_source & (t_own != 0) & (t_own != 6))
    def _():
        pl.semaphore_wait(token, 1)

    @pl.when(is_a_source)
    def _():
        for this in a_copies:
            this.start()
        for this in a_copies[:-1]:
            this.wait_send()

    @pl.when(is_a_source & (t_own != 5) & (t_own != 7) & (lag > t_own + 1))
    def _():
        pl.semaphore_signal(token, inc=1, device_id=(row, col - 1), device_id_type=MESH)

    def relay(condition, children, buffer, recvs, sends, pieces=large):
        @pl.when(condition)
        def _():
            for p, rows in enumerate(pieces):
                tile = buffer.at[rows]
                received(tile, recvs.at[p])
                send_all(children, tile, tile, sends, recvs.at[p])

    def take_b(q, carry):
        near = jnp.where(q % 3 == 0, 1, jnp.where(q % 3 == 1, 3, 2))
        source_row = jnp.where(q < 3, (x + near) % 4, jnp.where(q == 3, 5, 7))
        high = x + 3 - q
        turn = jnp.where(q == 3, 0, jnp.where(q == 4, 1, jnp.where(q == 5, 3, 2)))
        k = jnp.where(
            y == 0, source_row,
            jnp.where(y == 1, jnp.where(q < 3, high, (x + turn) % 4), 4 + 2 * q),
        )
        valid = jnp.where(
            y == 0, q < 5, jnp.where(y == 1, ((q >= 3) | (high >= 4)) & (q < 7), (y == 2) & (q < 2))
        )
        at = jnp.clip(k, 0, STEPS - 1)
        relay(valid & b_receives(at), b_children(at), bbuf.at[at], b_recv.at[at], b_send.at[at])
        return carry

    @pl.when((y < 3) & (col > 0))
    def _():
        lax.fori_loop(0, STEPS - 1, take_b, 0)

    def step(s, carry):
        @pl.when(even & (col < STEPS) & (s < 4))
        def _():
            first = jnp.where(s < 2, 2 * s, jnp.where(s == 2, 4, 5))
            second = jnp.minimum(jnp.where(s < 2, 2 * s + 1, s + 4), STEPS - 1)
            for t in (first, second):
                relay(a_receives(t), a_children(t), abuf.at[t], a_recv.at[t], a_send.at[t])

        lk = s - col
        k = s - lag
        lk_at, k_at = jnp.maximum(lk, 0), jnp.maximum(k, 0)
        mine = lag + col == s
        from_col = (lk >= 0) & (lag != lk) & ((lk < 4) | (y < 3))
        from_row = (k >= 0) & (col > k)
        use_col = (lk >= 0) & (lag > lk)

        to_col, to_row = col_children(lk_at), row_children(k_at)

        @pl.when(mine)
        def _():
            rounded = o_ref[...].astype(BF16)
            hbuf[...] = dot(ut[...], rounded).astype(BF16)
            ybuf[...] = (dot(hbuf[...], v_ref[...]) * inv[...]).astype(BF16)
            for p, rows in enumerate(parts):
                turned = dot(u_ref[rows, :], ybuf[...]).astype(BF16)
                answer = dot(turned, vt[...])
                o_ref[rows, :] = answer
                solved[rows, :] = answer.astype(BF16)
                src = solved.at[rows]
                send_all(
                    to_col, src, xcol.at[lk_at, rows], col_send.at[lk_at], col_recv.at[lk_at, p]
                )
                send_all(
                    to_row, src, xrow.at[k_at, rows], row_send.at[k_at], row_recv.at[k_at, p]
                )

        relay(from_row, to_row, xrow.at[k_at], row_recv.at[k_at], row_send.at[k_at], parts)

        @pl.when(from_row)
        def _():
            for p, rows in enumerate(large):
                received(bbuf.at[k_at, rows], b_recv.at[k_at, p])
            for p, rows in enumerate(parts):
                o_ref[rows, :] -= dot(xrow[k_at, rows, :], bbuf[k_at])

        @pl.when(use_col & ~even)
        def _():
            for p, rows in enumerate(large):
                received(abuf.at[lk_at, rows], a_recv.at[lk_at, p])

        @pl.when(from_col)
        def _():
            for p, rows in enumerate(parts):
                tile = xcol.at[lk_at, rows]
                received(tile, col_recv.at[lk_at, p])
                send_all(to_col, tile, tile, col_send.at[lk_at], col_recv.at[lk_at, p])

                @pl.when(use_col)
                def _():
                    o_ref[...] -= dot(abuf[lk_at, :, rows], xcol[lk_at, rows, :])

        return carry

    lax.fori_loop(0, STEPS, step, 0)

    sent_all(b_children(b_own), bbuf.at[b_own], b_send.at[b_own], is_b_source)

    @pl.when(is_a_source)
    def _():
        a_copies[-1].wait_send()

    def drain(s, carry):
        sent_all(a_children(s), abuf.at[s], a_send.at[s], a_receives(s))
        sent_all(b_children(s), bbuf.at[s], b_send.at[s], b_receives(s))
        lk = s - col
        k = s - lag
        lk_at, k_at = jnp.maximum(lk, 0), jnp.maximum(k, 0)
        source = lag + col == s
        from_col = (lk >= 0) & ((lk < 4) | (y < 3))
        from_row = (k >= 0) & (col >= k)
        sent_all(col_children(lk_at), xcol.at[lk_at], col_send.at[lk_at], from_col)
        sent_all(row_children(k_at), xrow.at[k_at], row_send.at[k_at], from_row)
        return carry

    lax.fori_loop(0, STEPS, drain, 0)


def per_device(right_side, upper_left, upper_right, vectors_left, vectors_right, values_left, values_right):
    size = right_side.shape[0]
    tile = pltpu.VMEM((size, size), BF16)
    tiles = pltpu.VMEM((STEPS, size, size), BF16)
    sems = pltpu.SemaphoreType.DMA
    vmem = pl.BlockSpec(memory_space=pltpu.VMEM)
    return pl.pallas_call(
        kernel,
        out_shape=jax.ShapeDtypeStruct((size, size), F32),
        in_specs=[pl.BlockSpec(memory_space=pl.ANY)] * 7,
        out_specs=vmem,
        scratch_shapes=[
            tile, tile, pltpu.VMEM((1, size), F32), pltpu.VMEM((1, size), F32),
            tile, tile, pltpu.VMEM((size, size), F32), tile, tile, tile,
            tiles, tiles, tiles, tiles,
            sems((STEPS, CHUNKS)), sems((STEPS, CHUNKS)), sems((STEPS, CHUNKS)), sems((STEPS, CHUNKS)),
            sems((STEPS, 5)), sems((STEPS, 2)), sems((STEPS, 2)), sems((STEPS, 4)),
            sems((CHUNKS,)), sems((5,)),
            pltpu.SemaphoreType.REGULAR,
        ],
        compiler_params=pltpu.CompilerParams(
            collective_id=0, has_side_effects=True, vmem_limit_bytes=67043328
        ),
        name="sylvester",
    )(
        right_side, upper_left, upper_right, vectors_left, vectors_right,
        values_left.reshape(1, size), values_right.reshape(1, size),
    )


def solution(mesh):
    in_specs = (
        P("row", "col"),
        P("row", "col"),
        P("row", "col"),
        P("row", None),
        P("col", None),
        P("row"),
        P("col"),
    )
    return jax.shard_map(
        per_device, mesh=mesh, in_specs=in_specs, out_specs=P("row", "col"), check_vma=False
    )
```
